32 devices in a mesh: dp: 16 (over z, y, x), mp: 2 (over core).
Axes of the slice: x: 2, y: 2, z: 4, core: 2. Of those that a mesh axis runs over, the one named last changes fastest.
Arguments:
- gradient: bfloat16 [2, 8, 512, 512], P('mp', None, 'dp'), may hold values from -54 to 54
- owners: int32 [2, 8], P('mp'), may hold values from 0 to 15, as said below
- left_stats: float32 [2, 16, 512, 512], P('mp', 'dp'), may hold values from -0.2 to 20.2
- right_stats: float32 [2, 16, 512, 512], P('mp', 'dp'), may hold values from -0.2 to 20.2
- left_roots_old: bfloat16 [2, 16, 512, 512], P('mp', 'dp'), may hold values from -0.1 to 1.5
- right_roots_old: bfloat16 [2, 16, 512, 512], P('mp', 'dp'), may hold values from -0.1 to 1.5
Outputs:
- update: bfloat16 [2, 8, 512, 512], P('mp', None, 'dp')
- left_roots: bfloat16 [2, 16, 512, 512], P('mp', 'dp')
- right_roots: bfloat16 [2, 16, 512, 512], P('mp', 'dp')
The draws below stay inside these ranges and needn't reach their ends.
Inputs may be any that keep to these rules, and one draw needn't show every extreme that they name: In each row the 8 owners are distinct. Owner o holds a block of row m exactly when owner (o + 8) mod 16 of row m holds none, and exactly when owner o of row (m + 1) mod 2 holds none.
All inputs are finite; a program needn't handle non-finite values.
Results may differ from the reference program's by a relative error of at most 0.0067.
Values may be sent and summed in bfloat16 or wider, within the bound.
A program may use at most 64 MiB of HBM per device.

```python
import math
import jax
import jax.numpy as jnp
from jax import lax

BLOCK = 512
ITERS = 2
NB = 8
N_DP = 16
N_MP = 2


def draw_gradient(key, part):
    key_noise, key_rows, key_cols = jax.random.split(key, 3)
    full_shape = (N_MP, NB, BLOCK, BLOCK)
    random_part = jax.random.truncated_normal(key_noise, -4.0, 4.0, full_shape, jnp.float32)
    upper_scale = 3.16
    row_scale = jnp.exp(jax.random.uniform(key_rows, (N_MP, NB, BLOCK, 1), jnp.float32, 0.0, math.log(upper_scale)))
    col_scale = jnp.exp(jax.random.uniform(key_cols, (N_MP, NB, 1, BLOCK), jnp.float32, 0.0, math.log(upper_scale)))
    rise_scale = (3.0 ** (jnp.arange(N_MP, dtype=jnp.float32) / (N_MP - 1))).reshape(N_MP, 1, 1, 1)
    return (0.25 * random_part * row_scale * col_scale * rise_scale).astype(jnp.bfloat16)


def draw_owners(key, part):
    half_dp = N_DP // 2
    half_mp = N_MP // 2
    key_bits, key_order = jax.random.split(jax.random.fold_in(key, 7))
    corner = jax.random.randint(key_bits, (half_mp, half_dp), 0, 2).astype(jnp.int32)
    corner_rows = jnp.concatenate([corner, corner], axis=0)
    upper_half = (jnp.arange(N_MP, dtype=jnp.int32) >= half_mp).astype(jnp.int32)[:, None]
    lower_busy = jnp.bitwise_xor(corner_rows, upper_half)
    busy_owner = jnp.arange(half_dp, dtype=jnp.int32)[None, :] + half_dp * (1 - lower_busy)
    scores = jax.random.randint(key_order, (N_MP, half_dp), 0, 1 << 20).astype(jnp.int32) * half_dp + jnp.arange(half_dp, dtype=jnp.int32)[None, :]
    ranking = jnp.argsort(scores, axis=1)
    return jnp.take_along_axis(busy_owner, ranking, axis=1).astype(jnp.int32)


def symmetric_draw(key, lower, upper, spread):
    key_diag, key_off = jax.random.split(key)
    diag_values = jnp.exp(jax.random.uniform(key_diag, (N_MP, N_DP, BLOCK), jnp.float32, math.log(lower), math.log(upper)))
    off_raw = jax.random.truncated_normal(key_off, -4.0, 4.0, (N_MP, N_DP, BLOCK, BLOCK), jnp.float32)
    off_sym = (off_raw + jnp.swapaxes(off_raw, 2, 3)) * (spread * lower / math.sqrt(BLOCK))
    return off_sym + diag_values[..., None] * jnp.eye(BLOCK, dtype=jnp.float32)


def draw_left_stats(key, part):
    return symmetric_draw(jax.random.fold_in(key, 11), 1.0, 10.0, 0.2)


def draw_right_stats(key, part):
    return symmetric_draw(jax.random.fold_in(key, 13), 1.0, 10.0, 0.2)


def draw_left_roots_old(key, part):
    return symmetric_draw(jax.random.fold_in(key, 17), 0.4, 1.2, 0.4).astype(jnp.bfloat16)


def draw_right_roots_old(key, part):
    return symmetric_draw(jax.random.fold_in(key, 19), 0.4, 1.2, 0.4).astype(jnp.bfloat16)


def setup_inputs(seed: int = 0) -> dict:
    streams_of = jax.random.split(jax.random.key(seed), 7)
    gradient = draw_gradient(jax.random.fold_in(streams_of[6], 71), 0)
    owners = draw_owners(jax.random.fold_in(streams_of[6], 71), 0)
    left_stats = draw_left_stats(jax.random.fold_in(streams_of[6], 71), 0)
    right_stats = draw_right_stats(jax.random.fold_in(streams_of[6], 71), 0)
    left_roots_old = draw_left_roots_old(jax.random.fold_in(streams_of[6], 71), 0)
    right_roots_old = draw_right_roots_old(jax.random.fold_in(streams_of[6], 71), 0)
    return {"gradient": gradient, "owners": owners, "left_stats": left_stats, "right_stats": right_stats, "left_roots_old": left_roots_old, "right_roots_old": right_roots_old}


stat_decay = 0.9
ridge_term = 0.001
tiny_term = 1e-06

def newton_root(statistic):
    dimension = statistic.shape[0]
    identity = jnp.eye(dimension, dtype=jnp.float32)
    shifted = statistic + ridge_term * identity
    norm_scale = jnp.sqrt(jnp.sum(shifted * shifted) + tiny_term)
    matrix = shifted / norm_scale
    iterate = identity
    for iteration in range(ITERS):
        factor = ((5.0 * identity - matrix) / 4.0).astype(jnp.bfloat16)
        if iteration == 0:
            iterate = norm_scale ** (-0.25) * lax.optimization_barrier(factor).astype(jnp.float32)
        else:
            iterate = jnp.dot(iterate.astype(jnp.bfloat16), factor, preferred_element_type=jnp.float32)
        if iteration + 1 < ITERS:
            factor_two = jnp.dot(factor, factor, preferred_element_type=jnp.float32).astype(jnp.bfloat16)
            factor_four = jnp.dot(factor_two, factor_two, preferred_element_type=jnp.float32).astype(jnp.bfloat16)
            matrix = jnp.dot(factor_four, matrix.astype(jnp.bfloat16), preferred_element_type=jnp.float32)
    return iterate.astype(jnp.bfloat16)

def reference(gradient, owners, left_stats, right_stats, left_roots_old, right_roots_old):
    shard_grid = jnp.broadcast_to(jnp.arange(N_MP, dtype=jnp.int32)[:, None], (N_MP, NB))
    block_grid = jnp.broadcast_to(jnp.arange(NB, dtype=jnp.int32)[None, :], (N_MP, NB))
    index_pairs = jnp.stack([shard_grid.reshape(-1), block_grid.reshape(-1)], axis=1)

    def per_block(indices):
        shard_id = indices[0]
        block_id = indices[1]
        owner_id = owners[shard_id, block_id]
        grad_block = gradient[shard_id, block_id]
        left_gram = jnp.dot(grad_block, grad_block.T, preferred_element_type=jnp.float32)
        right_gram = jnp.dot(grad_block.T, grad_block, preferred_element_type=jnp.float32)
        left_new = stat_decay * left_stats[shard_id, owner_id] + left_gram / BLOCK
        right_new = stat_decay * right_stats[shard_id, owner_id] + right_gram / BLOCK
        shaded = jnp.dot(grad_block, right_roots_old[shard_id, owner_id], preferred_element_type=jnp.float32).astype(jnp.bfloat16)
        direction = jnp.dot(left_roots_old[shard_id, owner_id], shaded, preferred_element_type=jnp.float32).astype(jnp.bfloat16)
        grad_square = jnp.sum(jnp.square(grad_block.astype(jnp.float32)))
        dir_square = jnp.sum(jnp.square(direction.astype(jnp.float32)))
        return (direction, grad_square, dir_square, newton_root(left_new), newton_root(right_new))
    directions, grad_squares, dir_squares, left_new_roots, right_new_roots = lax.map(per_block, index_pairs)
    grad_totals = lax.optimization_barrier(jnp.sum(grad_squares.reshape(N_MP, NB), axis=0))
    dir_totals = lax.optimization_barrier(jnp.sum(dir_squares.reshape(N_MP, NB), axis=0))
    graft_scale = jnp.sqrt(grad_totals / (dir_totals + tiny_term))
    update = (graft_scale[None, :, None, None] * directions.reshape(N_MP, NB, BLOCK, BLOCK).astype(jnp.float32)).astype(jnp.bfloat16)
    left_roots = jnp.zeros((N_MP, N_DP, BLOCK, BLOCK), jnp.bfloat16).at[shard_grid, owners].set(left_new_roots.reshape(N_MP, NB, BLOCK, BLOCK))
    right_roots = jnp.zeros((N_MP, N_DP, BLOCK, BLOCK), jnp.bfloat16).at[shard_grid, owners].set(right_new_roots.reshape(N_MP, NB, BLOCK, BLOCK))
    return (update, left_roots, right_roots)
```

```python
import functools

import jax
import jax.numpy as jnp
from jax import lax
from jax.experimental import pallas as pl
from jax.experimental.pallas import tpu as pltpu
from jax.sharding import PartitionSpec as P

ITERS = 2

stat_decay = 0.9
ridge_term = 0.001
tiny_term = 1e-06

MESH = pl.DeviceIdType.MESH


def mm(a, b, dims=((1,), (0,))):
    return lax.dot_general(a, b, (dims, ((), ())), preferred_element_type=jnp.float32)


def eye(n):
    rows = lax.broadcasted_iota(jnp.int32, (n, n), 0)
    cols = lax.broadcasted_iota(jnp.int32, (n, n), 1)
    return rows == cols


def newton_root(shifted):
    diag = eye(shifted.shape[0])
    scale = jnp.sqrt(jnp.sum(shifted * shifted, keepdims=True) + tiny_term)
    matrix = shifted / scale
    iterate = None
    for k in range(ITERS):
        factor = ((jnp.where(diag, 5.0, 0.0) - matrix) / 4.0).astype(jnp.bfloat16)
        if k == 0:
            iterate = jnp.exp(-0.25 * jnp.log(scale)) * factor.astype(jnp.float32)
        else:
            iterate = mm(iterate.astype(jnp.bfloat16), factor)
        if k + 1 < ITERS:
            two = mm(factor, factor).astype(jnp.bfloat16)
            four = mm(two, two).astype(jnp.bfloat16)
            matrix = mm(four, matrix.astype(jnp.bfloat16))
    return iterate


def kernel(
    n_dp, n_mp,
    owners, grad_hbm, lstat_hbm, rstat_hbm, lroot_hbm, rroot_hbm,
    update_hbm, lout_hbm, rout_hbm,
    grad, lstat, rstat, lroot, rroot,
    outgoing, arrived, direction, returned, upd, lout, rout,
    norm_out, norm_in, row_out, row_in,
    load_sem, store_sem, gs_sem, gr_sem, ds_sem, dr_sem, ns_sem, nr_sem, rs_sem, rr_sem,
):
    me = lax.axis_index("dp")
    mine = lax.axis_index("mp")
    nb, rows, width = grad.shape
    half = n_dp // 2

    loads = [
        pltpu.make_async_copy(src, dst, load_sem.at[i])
        for i, (src, dst) in enumerate(
            [(grad_hbm, grad), (rroot_hbm, rroot), (lroot_hbm, lroot), (lstat_hbm, lstat), (rstat_hbm, rstat)]
        )
    ]
    for load in loads:
        load.start()

    barrier = pltpu.get_barrier_semaphore()

    def greet_dp(i, carry):
        pl.semaphore_signal(barrier, inc=1, device_id=(lax.rem(me + i, n_dp), mine), device_id_type=MESH)
        return carry

    def greet_mp(i, carry):
        pl.semaphore_signal(barrier, inc=1, device_id=(me, lax.rem(mine + i, n_mp)), device_id_type=MESH)
        return carry

    lax.fori_loop(1, n_dp, greet_dp, 0)
    lax.fori_loop(1, n_mp, greet_mp, 0)

    busy = lax.fori_loop(0, nb, lambda j, a: a + (owners[0, j] == me).astype(jnp.int32), 0)
    busy_f = busy.astype(jnp.float32)

    loads[0].wait()

    def arrange(c, carry):
        j = lax.fori_loop(
            0, nb, lambda b, a: jnp.where(lax.rem(owners[0, b], half) == c, b, a), 0
        )
        outgoing[c] = grad[j]
        return carry

    lax.fori_loop(0, half, arrange, 0)

    pl.semaphore_wait(barrier, n_dp - 1 + n_mp - 1)

    def send_grad(i):
        peer = lax.rem(me + i, n_dp)
        return pltpu.make_async_remote_copy(
            src_ref=outgoing.at[lax.rem(peer, half)], dst_ref=arrived.at[me],
            send_sem=gs_sem.at[peer], recv_sem=gr_sem.at[me],
            device_id=(peer, mine), device_id_type=MESH,
        )

    def take_grad(i):
        peer = lax.rem(me + i, n_dp)
        return pltpu.make_async_remote_copy(
            src_ref=outgoing.at[lax.rem(peer, half)], dst_ref=arrived.at[peer],
            send_sem=gs_sem.at[peer], recv_sem=gr_sem.at[peer],
            device_id=(peer, mine), device_id_type=MESH,
        )

    def send_dir(i):
        peer = lax.rem(me + i, n_dp)
        return pltpu.make_async_remote_copy(
            src_ref=direction.at[peer], dst_ref=returned.at[me],
            send_sem=ds_sem.at[peer], recv_sem=dr_sem.at[me],
            device_id=(peer, mine), device_id_type=MESH,
        )

    def take_dir(i):
        peer = lax.rem(me + i, n_dp)
        return pltpu.make_async_remote_copy(
            src_ref=direction.at[peer], dst_ref=returned.at[peer],
            send_sem=ds_sem.at[peer], recv_sem=dr_sem.at[peer],
            device_id=(peer, mine), device_id_type=MESH,
        )

    def send_norm(i):
        peer = lax.rem(me + i, n_dp)
        return pltpu.make_async_remote_copy(
            src_ref=norm_out, dst_ref=norm_in.at[me],
            send_sem=ns_sem.at[peer], recv_sem=nr_sem.at[me],
            device_id=(peer, mine), device_id_type=MESH,
        )

    def take_norm(i):
        peer = lax.rem(me + i, n_dp)
        return pltpu.make_async_remote_copy(
            src_ref=norm_out, dst_ref=norm_in.at[peer],
            send_sem=ns_sem.at[peer], recv_sem=nr_sem.at[peer],
            device_id=(peer, mine), device_id_type=MESH,
        )

    def send_row(i):
        peer = lax.rem(mine + i, n_mp)
        return pltpu.make_async_remote_copy(
            src_ref=row_out, dst_ref=row_in.at[mine],
            send_sem=rs_sem.at[peer], recv_sem=rr_sem.at[mine],
            device_id=(me, peer), device_id_type=MESH,
        )

    def take_row(i):
        peer = lax.rem(mine + i, n_mp)
        return pltpu.make_async_remote_copy(
            src_ref=row_out, dst_ref=row_in.at[peer],
            send_sem=rs_sem.at[peer], recv_sem=rr_sem.at[peer],
            device_id=(me, peer), device_id_type=MESH,
        )

    def each(count, action):
        def step(i, carry):
            action(i)
            return carry

        lax.fori_loop(1, count, step, 0)

    def joined(ref):
        if rows % 16 == 0:
            return ref[...].reshape(n_dp * rows, width)
        return ref[...].astype(jnp.float32).reshape(n_dp * rows, width).astype(jnp.bfloat16)

    def split(value):
        if rows % 16 == 0:
            return value.reshape(n_dp, rows, width)
        return value.astype(jnp.float32).reshape(n_dp, rows, width).astype(jnp.bfloat16)

    each(n_dp, lambda i: send_grad(i).start())
    arrived[me] = outgoing[lax.rem(me, half)]
    loads[1].wait()
    loads[2].wait()
    each(n_dp, lambda i: take_grad(i).wait_recv())

    block = joined(arrived)
    shaded = mm(block, rroot[...]).astype(jnp.bfloat16)
    moved = mm(lroot[...], shaded).astype(jnp.bfloat16)
    direction[...] = split(moved)
    each(n_dp, lambda i: send_dir(i).start())
    returned[me] = direction[me]

    block32 = block.astype(jnp.float32)
    moved32 = moved.astype(jnp.float32)
    g_sum = jnp.sum(block32 * block32, keepdims=True) * busy_f
    d_sum = jnp.sum(moved32 * moved32, keepdims=True) * busy_f
    sub = lax.broadcasted_iota(jnp.int32, (8, 128), 0)
    lane = lax.broadcasted_iota(jnp.int32, (8, 128), 1)
    norm_out[...] = jnp.where(sub < 4, g_sum, d_sum)
    each(n_dp, lambda i: send_norm(i).start())
    norm_in[me] = norm_out[...]

    diag = eye(width)

    def refresh(stat, gram, out):
        shifted = (stat_decay * stat[...] + gram / width) + jnp.where(diag, ridge_term, 0.0)
        root = newton_root(shifted)
        out[...] = jnp.where(busy > 0, root, 0.0).astype(jnp.bfloat16)

    loads[3].wait()
    refresh(lstat, mm(block, block, ((1,), (1,))), lout)
    lcopy = pltpu.make_async_copy(lout, lout_hbm, store_sem.at[0])
    lcopy.start()

    each(n_dp, lambda i: take_norm(i).wait_recv())
    row_out[...] = lax.fori_loop(
        0, nb, lambda j, a: jnp.where(lane == j, norm_in[owners[0, j]], a), jnp.zeros((8, 128), jnp.float32)
    )
    each(n_mp, lambda i: send_row(i).start())
    row_in[mine] = row_out[...]

    loads[4].wait()
    refresh(rstat, mm(block, block, ((0,), (0,))), rout)
    rcopy = pltpu.make_async_copy(rout, rout_hbm, store_sem.at[1])
    rcopy.start()

    each(n_mp, lambda i: take_row(i).wait_recv())
    totals = lax.fori_loop(0, n_mp, lambda i, a: a + row_in[i], jnp.zeros((8, 128), jnp.float32))
    graft = jnp.sqrt(totals[0:1] / (totals[4:5] + tiny_term))
    lane1 = lax.broadcasted_iota(jnp.int32, (1, 128), 1)

    each(n_dp, lambda i: take_dir(i).wait_recv())

    def finish(j, carry):
        factor = jnp.sum(jnp.where(lane1 == j, graft, 0.0), keepdims=True)
        upd[j] = (factor * returned[owners[0, j]].astype(jnp.float32)).astype(jnp.bfloat16)
        return carry

    lax.fori_loop(0, nb, finish, 0)
    ucopy = pltpu.make_async_copy(upd, update_hbm, store_sem.at[2])
    ucopy.start()

    each(n_dp, lambda i: send_grad(i).wait_send())
    each(n_dp, lambda i: send_dir(i).wait_send())
    each(n_dp, lambda i: send_norm(i).wait_send())
    each(n_mp, lambda i: send_row(i).wait_send())
    lcopy.wait()
    rcopy.wait()
    ucopy.wait()


def shards(n_dp, n_mp, gradient, owners, left_stats, right_stats, left_roots_old, right_roots_old):
    _, nb, rows, width = gradient.shape
    half = n_dp // 2
    any_spec = pl.BlockSpec(memory_space=pl.ANY)
    bf16, f32 = jnp.bfloat16, jnp.float32
    dma = pltpu.SemaphoreType.DMA
    square = jax.ShapeDtypeStruct((width, width), bf16)
    update, left, right = pl.pallas_call(
        functools.partial(kernel, n_dp, n_mp),
        out_shape=(jax.ShapeDtypeStruct((nb, rows, width), bf16), square, square),
        in_specs=[pl.BlockSpec(memory_space=pltpu.SMEM)] + [any_spec] * 5,
        out_specs=(any_spec,) * 3,
        scratch_shapes=[
            pltpu.VMEM((nb, rows, width), bf16),
            pltpu.VMEM((width, width), f32),
            pltpu.VMEM((width, width), f32),
            pltpu.VMEM((width, width), bf16),
            pltpu.VMEM((width, width), bf16),
            pltpu.VMEM((half, rows, width), bf16),
            pltpu.VMEM((n_dp, rows, width), bf16),
            pltpu.VMEM((n_dp, rows, width), bf16),
            pltpu.VMEM((n_dp, rows, width), bf16),
            pltpu.VMEM((nb, rows, width), bf16),
            pltpu.VMEM((width, width), bf16),
            pltpu.VMEM((width, width), bf16),
            pltpu.VMEM((8, 128), f32),
            pltpu.VMEM((n_dp, 8, 128), f32),
            pltpu.VMEM((8, 128), f32),
            pltpu.VMEM((n_mp, 8, 128), f32),
            dma((5,)), dma((3,)),
            dma((n_dp,)), dma((n_dp,)), dma((n_dp,)), dma((n_dp,)), dma((n_dp,)), dma((n_dp,)),
            dma((n_mp,)), dma((n_mp,)),
        ],
        compiler_params=pltpu.CompilerParams(
            collective_id=0, has_side_effects=True
        ),
    )(owners, gradient[0], left_stats[0, 0], right_stats[0, 0], left_roots_old[0, 0], right_roots_old[0, 0])
    return update[None], left[None, None], right[None, None]


def solution(mesh):
    return jax.shard_map(
        functools.partial(shards, mesh.shape["dp"], mesh.shape["mp"]),
        mesh=mesh,
        in_specs=(
            P("mp", None, "dp", None),
            P("mp", None),
            P("mp", "dp", None, None),
            P("mp", "dp", None, None),
            P("mp", "dp", None, None),
            P("mp", "dp", None, None),
        ),
        out_specs=(P("mp", None, "dp", None), P("mp", "dp", None, None), P("mp", "dp", None, None)),
        check_vma=False,
    )
```

```python
import functools

import jax
import jax.numpy as jnp
from jax import lax
from jax.experimental import pallas as pl
from jax.experimental.pallas import tpu as pltpu
from jax.sharding import PartitionSpec as P

ITERS = 2

stat_decay = 0.9
ridge_term = 0.001
tiny_term = 1e-06

MESH = pl.DeviceIdType.MESH


def mm(a, b, dims=((1,), (0,))):
    return lax.dot_general(a, b, (dims, ((), ())), preferred_element_type=jnp.float32)


def eye(n):
    rows = lax.broadcasted_iota(jnp.int32, (n, n), 0)
    cols = lax.broadcasted_iota(jnp.int32, (n, n), 1)
    return rows == cols


def newton_root(shifted):
    diag = eye(shifted.shape[0])
    scale = jnp.sqrt(jnp.sum(shifted * shifted, keepdims=True) + tiny_term)
    matrix = shifted / scale
    iterate = None
    for k in range(ITERS):
        factor = ((jnp.where(diag, 5.0, 0.0) - matrix) / 4.0).astype(jnp.bfloat16)
        if k == 0:
            iterate = jnp.exp(-0.25 * jnp.log(scale)) * factor.astype(jnp.float32)
        else:
            iterate = mm(iterate.astype(jnp.bfloat16), factor)
        if k + 1 < ITERS:
            two = mm(factor, factor).astype(jnp.bfloat16)
            four = mm(two, two).astype(jnp.bfloat16)
            matrix = mm(four, matrix.astype(jnp.bfloat16))
    return iterate


def kernel(
    n_dp, n_mp,
    owners, grad_hbm, lstat_hbm, rstat_hbm, lroot_hbm, rroot_hbm,
    upd, lout, rout,
    grad, lstat, rstat, roots,
    stay, go, outgoing, arrived, direction, returned,
    norm_out, norm_in, row_out, row_in,
    load_sem, swap_sem, gs_sem, gr_sem, gf_sem, ds_sem, dr_sem, df_sem,
    ns_sem, nr_sem, rs_sem, rr_sem,
):
    me = lax.axis_index("dp")
    mine = lax.axis_index("mp")
    nb, rows, width = grad.shape
    half = n_dp // 2
    quarter = half // 2
    side = mine // (n_mp // 2)
    partner = lax.rem(mine + n_mp // 2, n_mp)
    kept = lax.rem(side + me, 2)
    given = 1 - kept

    loads = [
        pltpu.make_async_copy(src, dst, load_sem.at[i])
        for i, (src, dst) in enumerate(
            [
                (grad_hbm, grad),
                (rroot_hbm, roots.at[0, 1]),
                (lroot_hbm, roots.at[0, 0]),
                (lstat_hbm, lstat),
                (rstat_hbm, rstat),
            ]
        )
    ]
    for load in loads:
        load.start()

    def each(first, last, action):
        def step(i, carry):
            action(i)
            return carry

        lax.fori_loop(first, last, step, 0)

    barrier = pltpu.get_barrier_semaphore()

    def greet(dp, mp):
        pl.semaphore_signal(barrier, inc=1, device_id=(dp, mp), device_id_type=MESH)

    each(1, n_dp, lambda i: greet(lax.rem(me + i, n_dp), mine))
    each(1, n_mp, lambda i: greet(me, lax.rem(mine + i, n_mp)))

    def holds(owner):
        return lax.fori_loop(0, nb, lambda j, a: jnp.where(owners[0, j] == owner, 1, a), 0)

    def block_of(corner):
        return lax.fori_loop(
            0, nb, lambda j, a: jnp.where(lax.rem(owners[0, j], half) == corner, j, a), 0
        )

    busy = holds(me)

    loads[0].wait()

    def arrange(i):
        go[i] = grad[block_of(2 * i + given)]
        stay[0, i] = grad[block_of(2 * i + kept)]

    each(0, quarter, arrange)

    def remote(src, dst, send, recv, dp, mp):
        return pltpu.make_async_remote_copy(
            src_ref=src, dst_ref=dst, send_sem=send, recv_sem=recv,
            device_id=(dp, mp), device_id_type=MESH,
        )

    pl.semaphore_wait(barrier, n_dp - 1 + n_mp - 1)

    swap = remote(go, stay.at[1], swap_sem.at[0], swap_sem.at[1], me, partner)
    swap.start()
    loads[1].wait()
    swap_r = remote(roots.at[0, 1], roots.at[1, 1], swap_sem.at[2], swap_sem.at[3], me, partner)
    loads[2].wait()
    swap_l = remote(roots.at[0, 0], roots.at[1, 0], swap_sem.at[4], swap_sem.at[5], me, partner)

    first = 1 - side

    def ahead(d):
        return lax.rem(me + side + 2 * d, n_dp)

    def behind(d):
        return lax.rem(me + 2 * n_dp - side - 2 * d, n_dp)

    def across(d):
        return lax.rem(me + 2 * n_dp - (1 - side) - 2 * d, n_dp)

    def grad_out(peer):
        return remote(outgoing.at[peer // 2], arrived.at[me], gs_sem.at[peer], gr_sem.at[me], peer, mine)

    def grad_in(peer):
        return remote(outgoing.at[peer // 2], arrived.at[peer], gs_sem.at[peer], gr_sem.at[peer], peer, mine)

    def grad_on(peer):
        return remote(arrived.at[peer], arrived.at[peer], gf_sem.at[peer], gr_sem.at[peer], me, partner)

    def dir_out(peer):
        return remote(direction.at[peer], returned.at[me], ds_sem.at[peer], dr_sem.at[me], peer, mine)

    def dir_in(peer):
        return remote(direction.at[peer], returned.at[peer], ds_sem.at[peer], dr_sem.at[peer], peer, mine)

    def dir_on(peer):
        return remote(returned.at[peer], returned.at[peer], df_sem.at[peer], dr_sem.at[peer], me, partner)

    def norm_to(peer):
        return remote(norm_out, norm_in.at[me], ns_sem.at[peer], nr_sem.at[me], peer, mine)

    def norm_from(peer):
        return remote(norm_out, norm_in.at[peer], ns_sem.at[peer], nr_sem.at[peer], peer, mine)

    def row_to(peer):
        return remote(row_out, row_in.at[mine], rs_sem.at[peer], rr_sem.at[mine], me, peer)

    def row_from(peer):
        return remote(row_out, row_in.at[peer], rs_sem.at[peer], rr_sem.at[peer], me, peer)

    def joined(value):
        if rows % 16 == 0:
            return value.reshape(n_dp * rows, width)
        return value.astype(jnp.float32).reshape(n_dp * rows, width).astype(jnp.bfloat16)

    def split(value):
        if rows % 16 == 0:
            return value.reshape(n_dp, rows, width)
        return value.astype(jnp.float32).reshape(n_dp, rows, width).astype(jnp.bfloat16)

    swap.wait_recv()

    def dispatch(d):
        peer = ahead(d)
        outgoing[peer // 2] = stay[1 - holds(peer), lax.rem(peer // 2, quarter)]
        grad_out(peer).start()

    each(first, half, dispatch)
    swap_r.start()
    swap_l.start()

    @pl.when(side == 0)
    def _():
        arrived[me] = stay[1 - busy, lax.rem(me // 2, quarter)]
        grad_on(me).start()

    def pass_grad(d):
        grad_in(behind(d)).wait_recv()
        grad_on(behind(d)).start()

    each(first, half, pass_grad)
    swap_r.wait_recv()
    swap_l.wait_recv()
    each(0, half, lambda d: grad_on(across(d)).wait_recv())

    block = joined(arrived[...])
    shaded = mm(block, roots[1 - busy, 1]).astype(jnp.bfloat16)
    moved = mm(roots[1 - busy, 0], shaded).astype(jnp.bfloat16)
    direction[...] = split(moved)
    block32 = block.astype(jnp.float32)
    moved32 = moved.astype(jnp.float32)
    g_sum = jnp.sum(block32 * block32, keepdims=True)
    d_sum = jnp.sum(moved32 * moved32, keepdims=True)
    sub = lax.broadcasted_iota(jnp.int32, (2, 128), 0)
    lane = lax.broadcasted_iota(jnp.int32, (2, 128), 1)
    norm_out[...] = jnp.where(sub == 0, g_sum, d_sum)
    each(1, n_dp, lambda i: norm_to(lax.rem(me + i, n_dp)).start())
    each(first, half, lambda d: dir_out(ahead(d)).start())
    norm_in[me] = norm_out[...]
    returned[me] = direction[me]

    diag = eye(width)

    def refresh(stat, gram, out):
        shifted = (stat_decay * stat[...] + gram / width) + jnp.where(diag, ridge_term, 0.0)
        root = newton_root(shifted)
        out[...] = jnp.where(busy > 0, root, 0.0).astype(jnp.bfloat16)

    def pass_dir(d):
        dir_in(behind(d)).wait_recv()
        dir_on(behind(d)).start()

    loads[3].wait()
    refresh(lstat, mm(block, block, ((1,), (1,))), lout)

    each(1, n_dp, lambda i: norm_from(lax.rem(me + i, n_dp)).wait_recv())
    row_out[...] = lax.fori_loop(
        0, nb, lambda j, a: jnp.where(lane == j, norm_in[owners[0, j]], a), jnp.zeros((2, 128), jnp.float32)
    )
    each(1, n_mp, lambda i: row_to(lax.rem(mine + i, n_mp)).start())
    row_in[mine] = row_out[...]

    loads[4].wait()
    refresh(rstat, mm(block, block, ((0,), (0,))), rout)

    each(first, half, pass_dir)

    each(1, n_mp, lambda i: row_from(lax.rem(mine + i, n_mp)).wait_recv())
    totals = lax.fori_loop(0, n_mp, lambda i, a: a + row_in[i], jnp.zeros((2, 128), jnp.float32))
    graft = jnp.sqrt(totals[0:1] / (totals[1:2] + tiny_term))
    lane1 = lax.broadcasted_iota(jnp.int32, (1, 128), 1)

    each(1 - first, half, lambda d: dir_on(across(d)).wait_recv())

    def finish(j):
        factor = jnp.sum(jnp.where(lane1 == j, graft, 0.0), keepdims=True)
        upd[j] = (factor * returned[owners[0, j]].astype(jnp.float32)).astype(jnp.bfloat16)

    each(0, nb, finish)

    swap.wait_send()
    swap_r.wait_send()
    swap_l.wait_send()
    each(first, half, lambda d: grad_out(ahead(d)).wait_send())
    each(0, half, lambda d: grad_on(behind(d)).wait_send())
    each(first, half, lambda d: dir_out(ahead(d)).wait_send())
    each(first, half, lambda d: dir_on(behind(d)).wait_send())
    each(1, n_dp, lambda i: norm_to(lax.rem(me + i, n_dp)).wait_send())
    each(1, n_mp, lambda i: row_to(lax.rem(mine + i, n_mp)).wait_send())


def shards(n_dp, n_mp, gradient, owners, left_stats, right_stats, left_roots_old, right_roots_old):
    _, nb, rows, width = gradient.shape
    half = n_dp // 2
    hbm = pl.BlockSpec(memory_space=pltpu.HBM)
    vmem = pl.BlockSpec(memory_space=pltpu.VMEM)
    bf16, f32 = jnp.bfloat16, jnp.float32
    dma = pltpu.SemaphoreType.DMA
    square = jax.ShapeDtypeStruct((width, width), bf16)
    update, left, right = pl.pallas_call(
        functools.partial(kernel, n_dp, n_mp),
        out_shape=(jax.ShapeDtypeStruct((nb, rows, width), bf16), square, square),
        in_specs=[pl.BlockSpec(memory_space=pltpu.SMEM)] + [hbm] * 5,
        out_specs=(vmem,) * 3,
        scratch_shapes=[
            pltpu.VMEM((nb, rows, width), bf16),
            pltpu.VMEM((width, width), f32),
            pltpu.VMEM((width, width), f32),
            pltpu.VMEM((2, 2, width, width), bf16),
            pltpu.VMEM((2, half // 2, rows, width), bf16),
            pltpu.VMEM((half // 2, rows, width), bf16),
            pltpu.VMEM((half, rows, width), bf16),
            pltpu.VMEM((n_dp, rows, width), bf16),
            pltpu.VMEM((n_dp, rows, width), bf16),
            pltpu.VMEM((n_dp, rows, width), bf16),
            pltpu.VMEM((2, 128), f32),
            pltpu.VMEM((n_dp, 2, 128), f32),
            pltpu.VMEM((2, 128), f32),
            pltpu.VMEM((n_mp, 2, 128), f32),
            dma((5,)), dma((6,)),
            *[dma((n_dp,)) for _ in range(8)],
            dma((n_mp,)), dma((n_mp,)),
        ],
        compiler_params=pltpu.CompilerParams(
            collective_id=0, has_side_effects=True
        ),
    )(owners, gradient[0], left_stats[0, 0], right_stats[0, 0], left_roots_old[0, 0], right_roots_old[0, 0])
    return update[None], left[None, None], right[None, None]


def solution(mesh):
    return jax.shard_map(
        functools.partial(shards, mesh.shape["dp"], mesh.shape["mp"]),
        mesh=mesh,
        in_specs=(
            P("mp", None, "dp", None),
            P("mp", None),
            P("mp", "dp", None, None),
            P("mp", "dp", None, None),
            P("mp", "dp", None, None),
            P("mp", "dp", None, None),
        ),
        out_specs=(P("mp", None, "dp", None), P("mp", "dp", None, None), P("mp", "dp", None, None)),
        check_vma=False,
    )
```

```python
import functools

import jax
import jax.numpy as jnp
from jax import lax
from jax.experimental import pallas as pl
from jax.experimental.pallas import tpu as pltpu
from jax.sharding import PartitionSpec as P

ITERS = 2

stat_decay = 0.9
ridge_term = 0.001
tiny_term = 1e-06

MESH = pl.DeviceIdType.MESH


def mm(a, b, dims=((1,), (0,))):
    return lax.dot_general(a, b, (dims, ((), ())), preferred_element_type=jnp.float32)


def eye(n):
    rows = lax.broadcasted_iota(jnp.int32, (n, n), 0)
    cols = lax.broadcasted_iota(jnp.int32, (n, n), 1)
    return rows == cols


def newton_root(shifted):
    diag = eye(shifted.shape[0])
    scale = jnp.sqrt(jnp.sum(shifted * shifted, keepdims=True) + tiny_term)
    matrix = shifted / scale
    iterate = None
    for k in range(ITERS):
        factor = ((jnp.where(diag, 5.0, 0.0) - matrix) / 4.0).astype(jnp.bfloat16)
        if k == 0:
            iterate = jnp.exp(-0.25 * jnp.log(scale)) * factor.astype(jnp.float32)
        else:
            iterate = mm(iterate.astype(jnp.bfloat16), factor)
        if k + 1 < ITERS:
            two = mm(factor, factor).astype(jnp.bfloat16)
            four = mm(two, two).astype(jnp.bfloat16)
            matrix = mm(four, matrix.astype(jnp.bfloat16))
    return iterate


def kernel(
    n_dp, n_mp,
    owners, grad_hbm, lstat_hbm, rstat_hbm, lroot_hbm, rroot_hbm,
    upd, lout, rout,
    grad, lstat, rstat, roots,
    stay, go, outgoing, arrived, direction, returned,
    norm_out, norm_in, row_out, row_in,
    load_sem, swap_sem, gs_sem, gr_sem, gf_sem, ds_sem, dr_sem, df_sem,
    ns_sem, nr_sem, rs_sem, rr_sem,
):
    me = lax.axis_index("dp")
    mine = lax.axis_index("mp")
    nb, rows, width = grad.shape
    half = n_dp // 2
    quarter = half // 2
    side = mine // (n_mp // 2)
    partner = lax.rem(mine + n_mp // 2, n_mp)
    kept = lax.rem(side + me, 2)
    given = 1 - kept

    loads = [
        pltpu.make_async_copy(src, dst, load_sem.at[i])
        for i, (src, dst) in enumerate(
            [
                (grad_hbm, grad),
                (rroot_hbm, roots.at[0, 1]),
                (lroot_hbm, roots.at[0, 0]),
                (lstat_hbm, lstat),
                (rstat_hbm, rstat),
            ]
        )
    ]
    for load in loads:
        load.start()

    def each(first, last, action):
        def step(i, carry):
            action(i)
            return carry

        lax.fori_loop(first, last, step, 0)

    barrier = pltpu.get_barrier_semaphore()

    def greet(dp, mp):
        pl.semaphore_signal(barrier, inc=1, device_id=(dp, mp), device_id_type=MESH)

    each(1, n_dp, lambda i: greet(lax.rem(me + i, n_dp), mine))
    each(1, n_mp, lambda i: greet(me, lax.rem(mine + i, n_mp)))

    def holds(owner):
        return lax.fori_loop(0, nb, lambda j, a: jnp.where(owners[0, j] == owner, 1, a), 0)

    def block_of(corner):
        return lax.fori_loop(
            0, nb, lambda j, a: jnp.where(lax.rem(owners[0, j], half) == corner, j, a), 0
        )

    busy = holds(me)

    loads[0].wait()

    def arrange(i):
        go[i] = grad[block_of(2 * i + given)]
        stay[0, i] = grad[block_of(2 * i + kept)]

    each(0, quarter, arrange)

    def remote(src, dst, send, recv, dp, mp):
        return pltpu.make_async_remote_copy(
            src_ref=src, dst_ref=dst, send_sem=send, recv_sem=recv,
            device_id=(dp, mp), device_id_type=MESH,
        )

    pl.semaphore_wait(barrier, n_dp - 1 + n_mp - 1)

    swap = remote(go, stay.at[1], swap_sem.at[0], swap_sem.at[1], me, partner)
    swap.start()
    loads[1].wait()
    swap_r = remote(roots.at[0, 1], roots.at[1, 1], swap_sem.at[2], swap_sem.at[3], me, partner)
    loads[2].wait()
    swap_l = remote(roots.at[0, 0], roots.at[1, 0], swap_sem.at[4], swap_sem.at[5], me, partner)

    first = 1 - side

    def ahead(d):
        return lax.rem(me + side + 2 * d, n_dp)

    def behind(d):
        return lax.rem(me + 2 * n_dp - side - 2 * d, n_dp)

    def across(d):
        return lax.rem(me + 2 * n_dp - (1 - side) - 2 * d, n_dp)

    def grad_out(peer):
        return remote(outgoing.at[peer // 2], arrived.at[me], gs_sem.at[peer], gr_sem.at[me], peer, mine)

    def grad_in(peer):
        return remote(outgoing.at[peer // 2], arrived.at[peer], gs_sem.at[peer], gr_sem.at[peer], peer, mine)

    def grad_on(peer):
        return remote(arrived.at[peer], arrived.at[peer], gf_sem.at[peer], gr_sem.at[peer], me, partner)

    def dir_out(peer):
        return remote(direction.at[peer], returned.at[me], ds_sem.at[peer], dr_sem.at[me], peer, mine)

    def dir_in(peer):
        return remote(direction.at[peer], returned.at[peer], ds_sem.at[peer], dr_sem.at[peer], peer, mine)

    def dir_on(peer):
        return remote(returned.at[peer], returned.at[peer], df_sem.at[peer], dr_sem.at[peer], me, partner)

    def norm_to(peer):
        return remote(norm_out, norm_in.at[me], ns_sem.at[peer], nr_sem.at[me], peer, mine)

    def norm_from(peer):
        return remote(norm_out, norm_in.at[peer], ns_sem.at[peer], nr_sem.at[peer], peer, mine)

    def row_to(peer):
        return remote(row_out, row_in.at[mine], rs_sem.at[peer], rr_sem.at[mine], me, peer)

    def row_from(peer):
        return remote(row_out, row_in.at[peer], rs_sem.at[peer], rr_sem.at[peer], me, peer)

    def joined(value):
        if rows % 16 == 0:
            return value.reshape(n_dp * rows, width)
        return value.astype(jnp.float32).reshape(n_dp * rows, width).astype(jnp.bfloat16)

    def split(value):
        if rows % 16 == 0:
            return value.reshape(n_dp, rows, width)
        return value.astype(jnp.float32).reshape(n_dp, rows, width).astype(jnp.bfloat16)

    swap.wait_recv()

    def dispatch(d):
        peer = ahead(d)
        outgoing[peer // 2] = stay[1 - holds(peer), lax.rem(peer // 2, quarter)]
        grad_out(peer).start()

    each(first, half, dispatch)
    swap_r.start()
    swap_l.start()

    @pl.when(side == 0)
    def _():
        arrived[me] = stay[1 - busy, lax.rem(me // 2, quarter)]
        grad_on(me).start()

    def pass_grad(d):
        grad_in(behind(d)).wait_recv()
        grad_on(behind(d)).start()

    each(first, half, pass_grad)
    swap_r.wait_recv()
    swap_l.wait_recv()
    each(0, half, lambda d: grad_on(across(d)).wait_recv())

    block = joined(arrived[...])
    shaded = mm(block, roots[1 - busy, 1]).astype(jnp.bfloat16)
    moved = mm(roots[1 - busy, 0], shaded).astype(jnp.bfloat16)
    direction[...] = split(moved)
    block32 = block.astype(jnp.float32)
    moved32 = moved.astype(jnp.float32)
    g_sum = jnp.sum(block32 * block32, keepdims=True)
    d_sum = jnp.sum(moved32 * moved32, keepdims=True)
    sub = lax.broadcasted_iota(jnp.int32, (2, 128), 0)
    lane = lax.broadcasted_iota(jnp.int32, (2, 128), 1)
    norm_out[...] = jnp.where(sub == 0, g_sum, d_sum)
    each(1, n_dp, lambda i: norm_to(lax.rem(me + i, n_dp)).start())
    each(first, half, lambda d: dir_out(ahead(d)).start())
    norm_in[me] = norm_out[...]
    returned[me] = direction[me]

    diag = eye(width)

    def refresh(stat, gram, out):
        shifted = (stat_decay * stat[...] + gram / width) + jnp.where(diag, ridge_term, 0.0)
        root = newton_root(shifted)
        out[...] = jnp.where(busy > 0, root, 0.0).astype(jnp.bfloat16)

    def pass_dir(d):
        dir_in(behind(d)).wait_recv()
        dir_on(behind(d)).start()

    loads[3].wait()
    refresh(lstat, mm(block, block, ((1,), (1,))), lout)

    loads[4].wait()
    refresh(rstat, mm(block, block, ((0,), (0,))), rout)

    each(1, n_dp, lambda i: norm_from(lax.rem(me + i, n_dp)).wait_recv())
    row_out[...] = lax.fori_loop(
        0, nb, lambda j, a: jnp.where(lane == j, norm_in[owners[0, j]], a), jnp.zeros((2, 128), jnp.float32)
    )
    each(1, n_mp, lambda i: row_to(lax.rem(mine + i, n_mp)).start())
    row_in[mine] = row_out[...]

    each(first, half, pass_dir)

    each(1, n_mp, lambda i: row_from(lax.rem(mine + i, n_mp)).wait_recv())
    totals = lax.fori_loop(0, n_mp, lambda i, a: a + row_in[i], jnp.zeros((2, 128), jnp.float32))
    graft = jnp.sqrt(totals[0:1] / (totals[1:2] + tiny_term))
    lane1 = lax.broadcasted_iota(jnp.int32, (1, 128), 1)

    each(1 - first, half, lambda d: dir_on(across(d)).wait_recv())

    def finish(j):
        factor = jnp.sum(jnp.where(lane1 == j, graft, 0.0), keepdims=True)
        upd[j] = (factor * returned[owners[0, j]].astype(jnp.float32)).astype(jnp.bfloat16)

    each(0, nb, finish)

    swap.wait_send()
    swap_r.wait_send()
    swap_l.wait_send()
    each(first, half, lambda d: grad_out(ahead(d)).wait_send())
    each(0, half, lambda d: grad_on(behind(d)).wait_send())
    each(first, half, lambda d: dir_out(ahead(d)).wait_send())
    each(first, half, lambda d: dir_on(behind(d)).wait_send())
    each(1, n_dp, lambda i: norm_to(lax.rem(me + i, n_dp)).wait_send())
    each(1, n_mp, lambda i: row_to(lax.rem(mine + i, n_mp)).wait_send())


def settle(update_in, left_in, right_in, update, left, right, a, b, c, sems):
    ins = [
        pltpu.make_async_copy(src, dst, sems.at[i])
        for i, (src, dst) in enumerate([(left_in, b), (right_in, c), (update_in, a)])
    ]
    outs = [
        pltpu.make_async_copy(src, dst, sems.at[3 + i])
        for i, (src, dst) in enumerate([(b, left), (c, right), (a, update)])
    ]
    for copy in ins:
        copy.start()
    for arrives, leaves in zip(ins, outs):
        arrives.wait()
        leaves.start()
    for copy in outs:
        copy.wait()


def shards(n_dp, n_mp, gradient, owners, left_stats, right_stats, left_roots_old, right_roots_old):
    _, nb, rows, width = gradient.shape
    half = n_dp // 2
    hbm = pl.BlockSpec(memory_space=pltpu.HBM)
    vmem = pl.BlockSpec(memory_space=pltpu.VMEM)
    bf16, f32 = jnp.bfloat16, jnp.float32
    dma = pltpu.SemaphoreType.DMA
    square = jax.ShapeDtypeStruct((width, width), bf16)
    update, left, right = pl.pallas_call(
        functools.partial(kernel, n_dp, n_mp),
        out_shape=(jax.ShapeDtypeStruct((nb, rows, width), bf16), square, square),
        in_specs=[pl.BlockSpec(memory_space=pltpu.SMEM)] + [hbm] * 5,
        out_specs=(vmem,) * 3,
        scratch_shapes=[
            pltpu.VMEM((nb, rows, width), bf16),
            pltpu.VMEM((width, width), f32),
            pltpu.VMEM((width, width), f32),
            pltpu.VMEM((2, 2, width, width), bf16),
            pltpu.VMEM((2, half // 2, rows, width), bf16),
            pltpu.VMEM((half // 2, rows, width), bf16),
            pltpu.VMEM((half, rows, width), bf16),
            pltpu.VMEM((n_dp, rows, width), bf16),
            pltpu.VMEM((n_dp, rows, width), bf16),
            pltpu.VMEM((n_dp, rows, width), bf16),
            pltpu.VMEM((2, 128), f32),
            pltpu.VMEM((n_dp, 2, 128), f32),
            pltpu.VMEM((2, 128), f32),
            pltpu.VMEM((n_mp, 2, 128), f32),
            dma((5,)), dma((6,)),
            *[dma((n_dp,)) for _ in range(8)],
            dma((n_mp,)), dma((n_mp,)),
        ],
        compiler_params=pltpu.CompilerParams(
            collective_id=0, has_side_effects=True
        ),
    )(owners, gradient[0], left_stats[0, 0], right_stats[0, 0], left_roots_old[0, 0], right_roots_old[0, 0])
    update, left, right = pl.pallas_call(
        settle,
        out_shape=(jax.ShapeDtypeStruct((nb, rows, width), bf16), square, square),
        in_specs=[hbm] * 3,
        out_specs=(hbm,) * 3,
        scratch_shapes=[
            pltpu.VMEM((nb, rows, width), bf16),
            pltpu.VMEM((width, width), bf16),
            pltpu.VMEM((width, width), bf16),
            dma((6,)),
        ],
    )(update, left, right)
    return update[None], left[None, None], right[None, None]


def solution(mesh):
    return jax.shard_map(
        functools.partial(shards, mesh.shape["dp"], mesh.shape["mp"]),
        mesh=mesh,
        in_specs=(
            P("mp", None, "dp", None),
            P("mp", None),
            P("mp", "dp", None, None),
            P("mp", "dp", None, None),
            P("mp", "dp", None, None),
            P("mp", "dp", None, None),
        ),
        out_specs=(P("mp", None, "dp", None), P("mp", "dp", None, None), P("mp", "dp", None, None)),
        check_vma=False,
    )
```

```python
import functools

import jax
import jax.numpy as jnp
from jax import lax
from jax.experimental import pallas as pl
from jax.experimental.pallas import tpu as pltpu
from jax.sharding import PartitionSpec as P

ITERS = 2

stat_decay = 0.9
ridge_term = 0.001
tiny_term = 1e-06

MESH = pl.DeviceIdType.MESH


def mm(a, b, dims=((1,), (0,))):
    return lax.dot_general(a, b, (dims, ((), ())), preferred_element_type=jnp.float32)


def eye(n):
    rows = lax.broadcasted_iota(jnp.int32, (n, n), 0)
    cols = lax.broadcasted_iota(jnp.int32, (n, n), 1)
    return rows == cols


def newton_root(shifted):
    diag = eye(shifted.shape[0])
    scale = jnp.sqrt(jnp.sum(shifted * shifted, keepdims=True) + tiny_term)
    matrix = shifted / scale
    iterate = None
    for k in range(ITERS):
        factor = ((jnp.where(diag, 5.0, 0.0) - matrix) / 4.0).astype(jnp.bfloat16)
        if k == 0:
            iterate = jnp.exp(-0.25 * jnp.log(scale)) * factor.astype(jnp.float32)
        else:
            iterate = mm(iterate.astype(jnp.bfloat16), factor)
        if k + 1 < ITERS:
            two = mm(factor, factor).astype(jnp.bfloat16)
            four = mm(two, two).astype(jnp.bfloat16)
            matrix = mm(four, matrix.astype(jnp.bfloat16))
    return iterate


def kernel(
    n_dp, n_mp,
    owners, grad_hbm, lstat_hbm, rstat_hbm, lroot_hbm, rroot_hbm,
    update_hbm, lout_hbm, rout_hbm,
    upd, lout, rout, grad, lstat, rstat, roots,
    stay, go, outgoing, arrived, direction, returned,
    norm_out, norm_in, row_out, row_in,
    load_sem, store_sem, swap_sem, gs_sem, gr_sem, gf_sem, ds_sem, dr_sem, df_sem,
    ns_sem, nr_sem, rs_sem, rr_sem,
):
    me = lax.axis_index("dp")
    mine = lax.axis_index("mp")
    nb, rows, width = grad.shape
    half = n_dp // 2
    quarter = half // 2
    side = mine // (n_mp // 2)
    partner = lax.rem(mine + n_mp // 2, n_mp)
    kept = lax.rem(side + me, 2)
    given = 1 - kept

    loads = [
        pltpu.make_async_copy(src, dst, load_sem.at[i])
        for i, (src, dst) in enumerate(
            [
                (grad_hbm, grad),
                (rroot_hbm, roots.at[0, 1]),
                (lroot_hbm, roots.at[0, 0]),
                (lstat_hbm, lstat),
                (rstat_hbm, rstat),
            ]
        )
    ]
    for load in loads:
        load.start()

    def each(first, last, action):
        def step(i, carry):
            action(i)
            return carry

        lax.fori_loop(first, last, step, 0)

    barrier = pltpu.get_barrier_semaphore()

    def greet(dp, mp):
        pl.semaphore_signal(barrier, inc=1, device_id=(dp, mp), device_id_type=MESH)

    each(1, n_dp, lambda i: greet(lax.rem(me + i, n_dp), mine))
    each(1, n_mp, lambda i: greet(me, lax.rem(mine + i, n_mp)))

    def holds(owner):
        return lax.fori_loop(0, nb, lambda j, a: jnp.where(owners[0, j] == owner, 1, a), 0)

    def block_of(corner):
        return lax.fori_loop(
            0, nb, lambda j, a: jnp.where(lax.rem(owners[0, j], half) == corner, j, a), 0
        )

    busy = holds(me)

    loads[0].wait()

    def arrange(i):
        go[i] = grad[block_of(2 * i + given)]
        stay[0, i] = grad[block_of(2 * i + kept)]

    each(0, quarter, arrange)

    def remote(src, dst, send, recv, dp, mp):
        return pltpu.make_async_remote_copy(
            src_ref=src, dst_ref=dst, send_sem=send, recv_sem=recv,
            device_id=(dp, mp), device_id_type=MESH,
        )

    pl.semaphore_wait(barrier, n_dp - 1 + n_mp - 1)

    swap = remote(go, stay.at[1], swap_sem.at[0], swap_sem.at[1], me, partner)
    swap.start()
    loads[1].wait()
    swap_r = remote(roots.at[0, 1], roots.at[1, 1], swap_sem.at[2], swap_sem.at[3], me, partner)
    loads[2].wait()
    swap_l = remote(roots.at[0, 0], roots.at[1, 0], swap_sem.at[4], swap_sem.at[5], me, partner)

    first = 1 - side

    def ahead(d):
        return lax.rem(me + side + 2 * d, n_dp)

    def behind(d):
        return lax.rem(me + 2 * n_dp - side - 2 * d, n_dp)

    def across(d):
        return lax.rem(me + 2 * n_dp - (1 - side) - 2 * d, n_dp)

    def grad_out(peer):
        return remote(outgoing.at[peer // 2], arrived.at[me], gs_sem.at[peer], gr_sem.at[me], peer, mine)

    def grad_in(peer):
        return remote(outgoing.at[peer // 2], arrived.at[peer], gs_sem.at[peer], gr_sem.at[peer], peer, mine)

    def grad_on(peer):
        return remote(arrived.at[peer], arrived.at[peer], gf_sem.at[peer], gr_sem.at[peer], me, partner)

    def dir_out(peer):
        return remote(direction.at[peer], returned.at[me], ds_sem.at[peer], dr_sem.at[me], peer, mine)

    def dir_in(peer):
        return remote(direction.at[peer], returned.at[peer], ds_sem.at[peer], dr_sem.at[peer], peer, mine)

    def dir_on(peer):
        return remote(returned.at[peer], returned.at[peer], df_sem.at[peer], dr_sem.at[peer], me, partner)

    def norm_to(peer):
        return remote(norm_out, norm_in.at[me], ns_sem.at[peer], nr_sem.at[me], peer, mine)

    def norm_from(peer):
        return remote(norm_out, norm_in.at[peer], ns_sem.at[peer], nr_sem.at[peer], peer, mine)

    def row_to(peer):
        return remote(row_out, row_in.at[mine], rs_sem.at[peer], rr_sem.at[mine], me, peer)

    def row_from(peer):
        return remote(row_out, row_in.at[peer], rs_sem.at[peer], rr_sem.at[peer], me, peer)

    def joined(value):
        if rows % 16 == 0:
            return value.reshape(n_dp * rows, width)
        return value.astype(jnp.float32).reshape(n_dp * rows, width).astype(jnp.bfloat16)

    def split(value):
        if rows % 16 == 0:
            return value.reshape(n_dp, rows, width)
        return value.astype(jnp.float32).reshape(n_dp, rows, width).astype(jnp.bfloat16)

    swap.wait_recv()

    def dispatch(d):
        peer = ahead(d)
        outgoing[peer // 2] = stay[1 - holds(peer), lax.rem(peer // 2, quarter)]
        grad_out(peer).start()

    each(first, half, dispatch)
    swap_r.start()
    swap_l.start()

    @pl.when(side == 0)
    def _():
        arrived[me] = stay[1 - busy, lax.rem(me // 2, quarter)]
        grad_on(me).start()

    def pass_grad(d):
        grad_in(behind(d)).wait_recv()
        grad_on(behind(d)).start()

    each(first, half, pass_grad)
    swap_r.wait_recv()
    swap_l.wait_recv()
    each(0, half, lambda d: grad_on(across(d)).wait_recv())

    block = joined(arrived[...])
    block32 = block.astype(jnp.float32)
    g_sum = jnp.sum(block32 * block32, keepdims=True)
    shaded = mm(block, roots[1 - busy, 1]).astype(jnp.bfloat16)
    moved = mm(roots[1 - busy, 0], shaded).astype(jnp.bfloat16)
    direction[...] = split(moved)
    moved32 = moved.astype(jnp.float32)
    d_sum = jnp.sum(moved32 * moved32, keepdims=True)
    sub = lax.broadcasted_iota(jnp.int32, (2, 128), 0)
    lane = lax.broadcasted_iota(jnp.int32, (2, 128), 1)
    norm_out[...] = jnp.where(sub == 0, g_sum, d_sum)
    each(1, n_dp, lambda i: norm_to(lax.rem(me + i, n_dp)).start())
    each(first, half, lambda d: dir_out(ahead(d)).start())
    norm_in[me] = norm_out[...]
    returned[me] = direction[me]

    diag = eye(width)

    def refresh(stat, gram, out):
        shifted = (stat_decay * stat[...] + gram / width) + jnp.where(diag, ridge_term, 0.0)
        root = newton_root(shifted)
        out[...] = jnp.where(busy > 0, root, 0.0).astype(jnp.bfloat16)

    def pass_dir(d):
        dir_in(behind(d)).wait_recv()
        dir_on(behind(d)).start()

    loads[3].wait()
    refresh(lstat, mm(block, block, ((1,), (1,))), lout)
    lcopy = pltpu.make_async_copy(lout, lout_hbm, store_sem.at[0])
    lcopy.start()

    loads[4].wait()
    refresh(rstat, mm(block, block, ((0,), (0,))), rout)
    rcopy = pltpu.make_async_copy(rout, rout_hbm, store_sem.at[1])
    rcopy.start()

    each(1, n_dp, lambda i: norm_from(lax.rem(me + i, n_dp)).wait_recv())
    row_out[...] = lax.fori_loop(
        0, nb, lambda j, a: jnp.where(lane == j, norm_in[owners[0, j]], a), jnp.zeros((2, 128), jnp.float32)
    )
    each(1, n_mp, lambda i: row_to(lax.rem(mine + i, n_mp)).start())
    row_in[mine] = row_out[...]

    each(first, half, pass_dir)

    each(1, n_mp, lambda i: row_from(lax.rem(mine + i, n_mp)).wait_recv())
    totals = lax.fori_loop(0, n_mp, lambda i, a: a + row_in[i], jnp.zeros((2, 128), jnp.float32))
    graft = jnp.sqrt(totals[0:1] / (totals[1:2] + tiny_term))
    lane1 = lax.broadcasted_iota(jnp.int32, (1, 128), 1)

    each(1 - first, half, lambda d: dir_on(across(d)).wait_recv())

    def finish(j):
        factor = jnp.sum(jnp.where(lane1 == j, graft, 0.0), keepdims=True)
        upd[j] = (factor * returned[owners[0, j]].astype(jnp.float32)).astype(jnp.bfloat16)

    each(0, nb, finish)
    ucopy = pltpu.make_async_copy(upd, update_hbm, store_sem.at[2])
    ucopy.start()

    swap.wait_send()
    swap_r.wait_send()
    swap_l.wait_send()
    each(first, half, lambda d: grad_out(ahead(d)).wait_send())
    each(0, half, lambda d: grad_on(behind(d)).wait_send())
    each(first, half, lambda d: dir_out(ahead(d)).wait_send())
    each(first, half, lambda d: dir_on(behind(d)).wait_send())
    each(1, n_dp, lambda i: norm_to(lax.rem(me + i, n_dp)).wait_send())
    each(1, n_mp, lambda i: row_to(lax.rem(mine + i, n_mp)).wait_send())
    lcopy.wait()
    rcopy.wait()
    ucopy.wait()


def settle(update_in, left_in, right_in, update, left, right, a, b, c, sems):
    ins = [
        pltpu.make_async_copy(src, dst, sems.at[i])
        for i, (src, dst) in enumerate([(left_in, b), (right_in, c), (update_in, a)])
    ]
    outs = [
        pltpu.make_async_copy(src, dst, sems.at[3 + i])
        for i, (src, dst) in enumerate([(b, left), (c, right), (a, update)])
    ]
    for copy in ins:
        copy.start()
    for arrives, leaves in zip(ins, outs):
        arrives.wait()
        leaves.start()
    for copy in outs:
        copy.wait()


def shards(n_dp, n_mp, gradient, owners, left_stats, right_stats, left_roots_old, right_roots_old):
    _, nb, rows, width = gradient.shape
    half = n_dp // 2
    hbm = pl.BlockSpec(memory_space=pltpu.HBM)
    bf16, f32 = jnp.bfloat16, jnp.float32
    dma = pltpu.SemaphoreType.DMA
    square = jax.ShapeDtypeStruct((width, width), bf16)
    update, left, right = pl.pallas_call(
        functools.partial(kernel, n_dp, n_mp),
        out_shape=(jax.ShapeDtypeStruct((nb, rows, width), bf16), square, square),
        in_specs=[pl.BlockSpec(memory_space=pltpu.SMEM)] + [hbm] * 5,
        out_specs=(hbm,) * 3,
        scratch_shapes=[
            pltpu.VMEM((nb, rows, width), bf16),
            pltpu.VMEM((width, width), bf16),
            pltpu.VMEM((width, width), bf16),
            pltpu.VMEM((nb, rows, width), bf16),
            pltpu.VMEM((width, width), f32),
            pltpu.VMEM((width, width), f32),
            pltpu.VMEM((2, 2, width, width), bf16),
            pltpu.VMEM((2, half // 2, rows, width), bf16),
            pltpu.VMEM((half // 2, rows, width), bf16),
            pltpu.VMEM((half, rows, width), bf16),
            pltpu.VMEM((n_dp, rows, width), bf16),
            pltpu.VMEM((n_dp, rows, width), bf16),
            pltpu.VMEM((n_dp, rows, width), bf16),
            pltpu.VMEM((2, 128), f32),
            pltpu.VMEM((n_dp, 2, 128), f32),
            pltpu.VMEM((2, 128), f32),
            pltpu.VMEM((n_mp, 2, 128), f32),
            dma((5,)), dma((3,)), dma((6,)),
            *[dma((n_dp,)) for _ in range(8)],
            dma((n_mp,)), dma((n_mp,)),
        ],
        compiler_params=pltpu.CompilerParams(
            collective_id=0, has_side_effects=True
        ),
    )(owners, gradient[0], left_stats[0, 0], right_stats[0, 0], left_roots_old[0, 0], right_roots_old[0, 0])
    update, left, right = pl.pallas_call(
        settle,
        out_shape=(jax.ShapeDtypeStruct((nb, rows, width), bf16), square, square),
        in_specs=[hbm] * 3,
        out_specs=(hbm,) * 3,
        scratch_shapes=[
            pltpu.VMEM((nb, rows, width), bf16),
            pltpu.VMEM((width, width), bf16),
            pltpu.VMEM((width, width), bf16),
            dma((6,)),
        ],
    )(update, left, right)
    return update[None], left[None, None], right[None, None]


def solution(mesh):
    return jax.shard_map(
        functools.partial(shards, mesh.shape["dp"], mesh.shape["mp"]),
        mesh=mesh,
        in_specs=(
            P("mp", None, "dp", None),
            P("mp", None),
            P("mp", "dp", None, None),
            P("mp", "dp", None, None),
            P("mp", "dp", None, None),
            P("mp", "dp", None, None),
        ),
        out_specs=(P("mp", None, "dp", None), P("mp", "dp", None, None), P("mp", "dp", None, None)),
        check_vma=False,
    )
```
